32 devices in a mesh: rows: 4 (over y, core), chan: 8 (over z, x).
Axes of the slice: x: 2, y: 2, z: 4, core: 2. Of those that a mesh axis runs over, the one named last changes fastest.
Arguments:
- features: bfloat16 [1024, 16, 128], P('chan', 'rows'), may hold values from -6 to 6
- hidden: bfloat16 [1024, 16, 128], P('chan', 'rows'), may hold values from -1 to 1
- w_update: bfloat16 [3, 3, 1024, 2048], P(None, None, 'chan'), may hold values from -0.046875 to 0.046875
- w_reset: bfloat16 [3, 3, 1024, 2048], P(None, None, 'chan'), may hold values from -0.046875 to 0.046875
- w_cand: bfloat16 [3, 3, 1024, 2048], P(None, None, 'chan'), may hold values from -0.046875 to 0.046875
- b_update: float32 [1024], P('chan'), may hold values from -1 to 1
- b_reset: float32 [1024], P('chan'), may hold values from -1 to 1
- b_cand: float32 [1024], P('chan'), may hold values from -1 to 1
Outputs:
- new_hidden: bfloat16 [1024, 16, 128], P('chan', 'rows')
The draws below stay inside these ranges and needn't reach their ends.
All inputs are finite; a program needn't handle non-finite values.
Results may differ from the reference program's by a relative error of at most 0.0018.
Values may be sent and summed in bfloat16 or wider, within the bound.
A program may use at most 128 MiB of HBM per device.

```python
import jax
import jax.numpy as jnp
from jax import lax

C_IN = 1024
HID = 1024
COLS = 128
HEIGHT = 16


def level_of(own_key, extent, split, least, largest):
    factor_of, own = 1.0, jax.random.fold_in(own_key, 6)
    for position, parts in split:
        steps = jnp.exp(jax.random.uniform(jax.random.fold_in(own, position), (parts,), jnp.float32, least / len(split), largest / len(split)))
        factor_of = factor_of * jnp.repeat(steps, extent[position] // parts).reshape([-1 if axis == position else 1 for axis in range(len(extent))])
    return factor_of


def noise(key, shape, width, most, pieces=(), held_as=jnp.bfloat16):
    level = level_of(key, shape, pieces, -0.22, 0.18) if pieces else 1.0
    drawn = jax.random.normal(key, shape, jnp.float32) * width * level
    return jnp.minimum(jnp.maximum(drawn, -most), most).astype(held_as)


def setup_inputs(seed: int = 0) -> dict:
    arg_keys = jax.random.split(jax.random.key(seed), 9)
    features = noise(arg_keys[0], (C_IN, HEIGHT, COLS), 1.0, 6.0, ((0, 8), (1, 4)))
    hidden = jnp.clip(jax.random.uniform(arg_keys[1], (HID, HEIGHT, COLS), jnp.float32, -1.0, 1.0) * level_of(arg_keys[1], (HID, HEIGHT, COLS), ((0, 8), (1, 4)), -0.4, 0.0), -1.0, 1.0).astype(jnp.bfloat16)
    w_update = noise(arg_keys[2], (3, 3, HID, C_IN + HID), (9 * (C_IN + HID)) ** -0.5, 0.046875, ((2, 8),))
    w_reset = noise(arg_keys[3], (3, 3, HID, C_IN + HID), (9 * (C_IN + HID)) ** -0.5, 0.046875, ((2, 8),))
    w_cand = noise(arg_keys[4], (3, 3, HID, C_IN + HID), (9 * (C_IN + HID)) ** -0.5, 0.046875, ((2, 8),))
    b_update = jnp.clip(jax.random.uniform(arg_keys[5], (HID,), jnp.float32, -1.0, 1.0) * level_of(arg_keys[5], (HID,), ((0, 8),), -0.4, 0.0), -1.0, 1.0)
    b_reset = jnp.clip(jax.random.uniform(arg_keys[6], (HID,), jnp.float32, -1.0, 1.0) * level_of(arg_keys[6], (HID,), ((0, 8),), -0.4, 0.0), -1.0, 1.0)
    b_cand = jnp.clip(jax.random.uniform(arg_keys[7], (HID,), jnp.float32, -1.0, 1.0) * level_of(arg_keys[7], (HID,), ((0, 8),), -0.4, 0.0), -1.0, 1.0)
    return {"features": features, "hidden": hidden, "w_update": w_update, "w_reset": w_reset, "w_cand": w_cand, "b_update": b_update, "b_reset": b_reset, "b_cand": b_cand}


def conv_full(source, kernel):
    weights = jnp.transpose(kernel.astype(jnp.float32), (2, 3, 0, 1))
    result = lax.conv_general_dilated(source[None], weights, (1, 1), ((1, 1), (1, 1)), dimension_numbers=("NCHW", "OIHW", "NCHW"), precision=lax.Precision.HIGHEST)
    return result[0]


def reference(features, hidden, w_update, w_reset, w_cand, b_update, b_reset, b_cand):
    joined = jnp.concatenate([features, hidden], 0).astype(jnp.float32)
    update = jax.nn.sigmoid(conv_full(joined, w_update) + b_update[:, None, None])
    reset = jax.nn.sigmoid(conv_full(joined, w_reset) + b_reset[:, None, None])
    hidden_f = hidden.astype(jnp.float32)
    reset_hidden = (reset * hidden_f).astype(jnp.bfloat16)
    second = jnp.concatenate([features.astype(jnp.float32), reset_hidden.astype(jnp.float32)], 0)
    candidate = jnp.tanh(conv_full(second, w_cand) + b_cand[:, None, None])
    return ((1.0 - update) * hidden_f + update * candidate).astype(jnp.bfloat16)
```

```python
import functools

import jax
import jax.numpy as jnp
from jax import lax
from jax.experimental import pallas as pl
from jax.experimental.pallas import tpu as pltpu
from jax.sharding import PartitionSpec as P

MESH = pl.DeviceIdType.MESH
PAIR = 2
WIDE = 128
EDGE, INNER = 0, 1


def kernel(
    n_chan, n_rows, rows,
    features, hidden, b_update, b_reset, b_cand, w_update, w_reset, w_cand,
    out,
    raw, joined, rh, weights, acc, acc_cand, gate, bias,
    raw_sem, w_sem, send1, band1, rim1, send2, band2, rim2,
):
    cols = raw.shape[-1]
    channels = joined.shape[2]
    n = channels // n_chan
    lines = n_chan // PAIR
    me = lax.axis_index("chan")
    row = lax.axis_index("rows")
    line, pair = me // PAIR, me % PAIR
    has_up, has_down = line < lines - 1, line > 0
    has_above, has_below = row > 0, row < n_rows - 1
    eager = n % WIDE == 0
    f32 = jnp.float32

    raw_copies = [
        pltpu.make_async_copy(src, raw.at[i], raw_sem.at[i])
        for i, src in enumerate((features, hidden))
    ]
    w_copies = [
        pltpu.make_async_copy(src, weights.at[i], w_sem.at[i])
        for i, src in enumerate((w_reset, w_update, w_cand))
    ]
    for copy in raw_copies + w_copies:
        copy.start()

    def ident(l, p):
        return l * PAIR + p

    up, down, partner = ident(line + 1, pair), ident(line - 1, pair), ident(line, 1 - pair)
    barrier = pltpu.get_barrier_semaphore()

    def greet(there, target):
        @pl.when(there)
        def _():
            pl.semaphore_signal(barrier, inc=1, device_id=target, device_id_type=MESH)

    pl.semaphore_signal(barrier, inc=1, device_id={"chan": partner}, device_id_type=MESH)
    greet(has_up, {"chan": up})
    greet(has_down, {"chan": down})
    greet(has_above, {"rows": row - 1})
    greet(has_below, {"rows": row + 1})

    def slot(r):
        if r == -1 or r == rows:
            return rows + (r == rows)
        return {0: 0, rows - 1: 1}.get(r, r + 1)

    def block(c):
        return pl.ds(pl.multiple_of(c * n, n), n)

    mine = block(me)

    def iota(shape, axis):
        return lax.broadcasted_iota(jnp.int32, shape, axis)

    to_planes = jnp.concatenate(
        [
            (iota((n, n * rows), 0) * rows + r == iota((n, n * rows), 1)).astype(f32)
            for r in range(rows)
        ],
        0,
    ).astype(raw.dtype)
    for i, copy in enumerate(raw_copies):
        copy.wait()
        planes = jnp.dot(to_planes, raw[i], preferred_element_type=f32).astype(raw.dtype)
        for r in range(rows):
            joined[i, slot(r), mine] = planes[r * n : (r + 1) * n]

    pl.semaphore_wait(
        barrier,
        1
        + has_up.astype(jnp.int32)
        + has_down.astype(jnp.int32)
        + has_above.astype(jnp.int32)
        + has_below.astype(jnp.int32),
    )

    class Mover:
        def __init__(self, buf, send, band_sem, rim_sem):
            self.buf, self.send, self.band_sem, self.rim_sem = buf, send, band_sem, rim_sem
            self.kinds = range(buf.shape[0])

        def band(self, way, c, part, h):
            slots = pl.ds(0, 2) if part == EDGE else pl.ds(2, rows - 2)
            ref = self.buf.at[h, slots, block(c)]
            return pltpu.make_async_remote_copy(
                src_ref=ref,
                dst_ref=ref,
                send_sem=self.send.at[way, c, part, h],
                recv_sem=self.band_sem.at[c, part, h],
                device_id={"chan": (up, down, partner)[way]},
                device_id_type=MESH,
            )

        def rim(self, side, c, h):
            return pltpu.make_async_remote_copy(
                src_ref=self.buf.at[h, side, block(c)],
                dst_ref=self.buf.at[h, rows + 1 - side, block(c)],
                send_sem=self.send.at[3 + side, c, EDGE, h],
                recv_sem=self.rim_sem.at[side, c, h],
                device_id={"rows": row - 1 if side == 0 else row + 1},
                device_id_type=MESH,
            )

        def rims(self, c, h, act):
            @pl.when(has_above)
            def _():
                act(self.rim(0, c, h))

            @pl.when(has_below)
            def _():
                act(self.rim(1, c, h))

        def along(self, way, c, part, h, act):
            @pl.when((has_up, has_down)[way])
            def _():
                act(self.band(way, c, part, h))

        def begin(self, act, part):
            for h in self.kinds:
                self.along(0, me, part, h, act)
                self.along(1, me, part, h, act)
                act(self.band(2, me, part, h))
            if part == EDGE:
                for h in self.kinds:
                    self.rims(me, h, act)

        def pass_on(self, s, act, first):
            for part in (EDGE, INNER):
                for h in self.kinds:
                    for way, l in ((0, line - s), (1, line + s)):
                        @pl.when((l >= 0) & (l < lines))
                        def _():
                            c = ident(l, pair)
                            if first:
                                self.band(2, c, part, h).wait_recv()
                            self.along(way, c, part, h, act)
                            if part == EDGE or s > 1:
                                act(self.band(2, c, part, h))
                            if part == EDGE:
                                self.rims(c, h, act)

        def diagonal(self, act):
            for h in self.kinds:
                self.along(0, partner, INNER, h, act)
                self.along(1, partner, INNER, h, act)

        def across(self, s, act, first):
            for l in (line - s, line + s)[: 1 if s == 0 else 2]:
                @pl.when((l >= 0) & (l < lines))
                def _():
                    c = ident(l, 1 - pair)
                    for h in self.kinds:
                        if first:
                            self.band(2, c, EDGE, h).wait_recv()
                        self.rims(c, h, act)

        def rims_in(self, c):
            for h in self.kinds:
                @pl.when(has_below)
                def _():
                    self.rim(0, c, h).wait_recv()

                @pl.when(has_above)
                def _():
                    self.rim(1, c, h).wait_recv()

        def inner_in(self, c):
            for h in self.kinds:
                self.band(2, c, INNER, h).wait_recv()

        def finish(self):
            for part in (EDGE, INNER):
                self.begin(done, part)
            for s in range(1, lines):
                self.pass_on(s, done, False)
            self.diagonal(done)
            for s in range(lines):
                self.across(s, done, False)

    def start(copy):
        copy.start()

    def done(copy):
        copy.wait_send()

    def sides(s, body):
        @pl.loop(0, 2)
        def _(j):
            l = line + (2 * j - 1) * s

            @pl.when((l >= 0) & (l < lines))
            def _():
                body(l)

    first, second = Mover(joined, send1, band1, rim1), Mover(rh, send2, band2, rim2)
    for part in (EDGE, INNER):
        first.begin(start, part)

    for there, r in ((has_above, -1), (has_below, rows)):
        @pl.when(jnp.logical_not(there))
        def _():
            for buf in (joined, rh):
                for h in range(buf.shape[0]):
                    buf[h, slot(r)] = jnp.zeros((channels, cols), buf.dtype)

    diagonal = iota((n, n), 0) == iota((n, n), 1)
    for i, ref in enumerate((b_reset, b_update, b_cand)):
        column = jnp.sum(jnp.where(diagonal, ref[...], 0.0), axis=1, keepdims=True)
        bias[i] = jnp.broadcast_to(column, (n, cols))
    acc_cand[...] = jnp.zeros_like(acc_cand)
    if not eager:
        acc[...] = jnp.zeros_like(acc)

    def product(gates, count, sources, at, width):
        left, right = [], []
        for a in range(3):
            for offset, buf, h in sources:
                kw = pl.ds(pl.multiple_of(offset + at, WIDE), width)
                ks = pl.ds(pl.multiple_of(at, WIDE), width)
                left.append(
                    weights[pl.ds(gates, count), a, :, :, kw].reshape(count * 3 * n, width)
                )
                right.append(
                    jnp.concatenate([buf[h, slot(r + a - 1), ks] for r in range(rows)], 1)
                )
        return jnp.dot(
            jnp.concatenate(left, 1),
            jnp.concatenate(right, 0),
            preferred_element_type=f32,
        )

    both = ((0, joined, 0), (channels, joined, 1))
    size = 3 * n

    def gates_on(c):
        acc[...] += product(0, 2, both, c * n, n)

    def reset_on(c):
        acc[pl.ds(0, size)] += product(0, 1, both, c * n, n)

    def update_on(c):
        acc[pl.ds(size, size)] += product(1, 1, both, c * n, n)

    def old_on(at, width):
        acc_cand[...] += product(2, 1, ((0, joined, 0),), at, width)

    def new_on(at, width):
        acc_cand[...] += product(2, 1, ((channels, rh, 0),), at, width)

    last = sorted({1, lines - 1})

    def near(s):
        def body(l):
            c = ident(l, pair)
            first.rims_in(c)
            gates_on(c)

        sides(s, body)

    def far(s, compute):
        def body(l):
            c = ident(l, 1 - pair)
            first.inner_in(c)
            first.rims_in(c)
            compute(c)

        sides(s, body)

    for s in range(1, lines):
        first.pass_on(s, start, True)
        if s == max(1, lines - 2):
            if s == 1:
                first.inner_in(partner)
            first.diagonal(start)
        first.across(s - 1, start, True)
        if s == 1:
            if lines > 3:
                first.inner_in(partner)
            w_copies[0].wait()
            w_copies[1].wait()
            if eager:
                first.rims_in(me)
                acc[...] = product(0, 2, both, me * n, n)
                first.rims_in(partner)
                gates_on(partner)
        elif eager:
            near(s - 1)
            if s > 2:
                far(s - 1, gates_on)
    first.across(lines - 1, start, True)
    if eager:
        near(lines - 1)
        for s in last:
            far(s, reset_on)
    else:
        for s in range(1, lines):
            sides(s, lambda l: first.inner_in(ident(l, 1 - pair)))

        @pl.loop(0, n_chan)
        def _(c):
            first.rims_in(c)

        @pl.loop(0, channels // WIDE)
        def _(g):
            acc[...] += product(0, 2, both, g * WIDE, WIDE)

    lane = iota((n, cols), 1)

    def folded(ref, i, r):
        cells = pl.ds(r * cols, cols)
        low = pltpu.roll(ref[pl.ds(i * size, n), cells], 1, 1)
        mid = ref[pl.ds(i * size + n, n), cells]
        high = pltpu.roll(ref[pl.ds(i * size + 2 * n, n), cells], cols - 1, 1)
        return jnp.where(lane == 0, 0.0, low) + mid + jnp.where(lane == cols - 1, 0.0, high)

    def own_hidden(r):
        return joined[1, slot(r), mine].astype(f32)

    for part, inside in ((EDGE, (0, rows - 1)), (INNER, range(1, rows - 1))):
        for r in inside:
            reset = jax.nn.sigmoid(folded(acc, 0, r) + bias[0])
            rh[0, slot(r), mine] = (reset * own_hidden(r)).astype(rh.dtype)
        second.begin(start, part)

    if eager:
        for s in last:
            sides(s, lambda l: update_on(ident(l, 1 - pair)))
    w_copies[2].wait()

    def older():
        width = PAIR * n if eager else WIDE

        @pl.loop(0, channels // width)
        def _(g):
            old_on(g * width, width)

        for r in range(rows):
            gate[r] = jax.nn.sigmoid(folded(acc, 1, r) + bias[1])

    def both_on(l):
        for p in range(PAIR):
            second.rims_in(ident(l, p))
        new_on(l * PAIR * n, PAIR * n)

    def both_far(s):
        def body(l):
            second.inner_in(ident(l, 1 - pair))
            both_on(l)

        sides(s, body)

    for s in range(1, lines):
        second.pass_on(s, start, True)
        if s == max(1, lines - 2):
            if s == 1:
                second.inner_in(partner)
            second.diagonal(start)
        second.across(s - 1, start, True)
        if s == 1:
            if lines > 3:
                second.inner_in(partner)
            older()
            if eager:
                both_on(line)
        elif eager and s > 2:
            both_far(s - 1)
    second.across(lines - 1, start, True)
    if eager:
        for s in last:
            both_far(s)
    else:
        for s in range(1, lines):
            sides(s, lambda l: second.inner_in(ident(l, 1 - pair)))

        @pl.loop(0, n_chan)
        def _(c):
            second.rims_in(c)

        @pl.loop(0, channels // WIDE)
        def _(g):
            new_on(g * WIDE, WIDE)

    fresh = []
    for r in range(rows):
        candidate = jnp.tanh(folded(acc_cand, 0, r) + bias[2])
        update = gate[r]
        fresh.append(((1.0 - update) * own_hidden(r) + update * candidate).astype(out.dtype))
    from_planes = jnp.concatenate(
        [
            (iota((n * rows, n), 0) == iota((n * rows, n), 1) * rows + r).astype(f32)
            for r in range(rows)
        ],
        1,
    ).astype(out.dtype)
    out[...] = jnp.dot(
        from_planes, jnp.concatenate(fresh, 0), preferred_element_type=f32
    ).astype(out.dtype)
    first.finish()
    second.finish()


def per_device(n_chan, n_rows, features, hidden, w_update, w_reset, w_cand, b_update, b_reset, b_cand):
    n, rows, cols = features.shape
    band = rows * cols
    channels = n * n_chan
    bf16, f32 = jnp.bfloat16, jnp.float32
    vmem = pl.BlockSpec(memory_space=pltpu.VMEM)
    hbm = pl.BlockSpec(memory_space=pl.ANY)
    dma = pltpu.SemaphoreType.DMA
    result = pl.pallas_call(
        functools.partial(kernel, n_chan, n_rows, rows),
        out_shape=jax.ShapeDtypeStruct((n * rows, cols), bf16),
        in_specs=[hbm] * 2 + [vmem] * 3 + [hbm] * 3,
        out_specs=vmem,
        scratch_shapes=[
            pltpu.VMEM((2, n * rows, cols), bf16),
            pltpu.VMEM((2, rows + 2, channels, cols), bf16),
            pltpu.VMEM((1, rows + 2, channels, cols), bf16),
            pltpu.VMEM((3,) + w_update.shape, bf16),
            pltpu.VMEM((6 * n, band), f32),
            pltpu.VMEM((3 * n, band), f32),
            pltpu.VMEM((rows, n, cols), f32),
            pltpu.VMEM((3, n, cols), f32),
            dma((2,)),
            dma((3,)),
            dma((5, n_chan, 2, 2)),
            dma((n_chan, 2, 2)),
            dma((2, n_chan, 2)),
            dma((5, n_chan, 2, 1)),
            dma((n_chan, 2, 1)),
            dma((2, n_chan, 1)),
        ],
        compiler_params=pltpu.CompilerParams(
            collective_id=0, has_side_effects=True, vmem_limit_bytes=60 * 1024 * 1024
        ),
    )(
        features.reshape(n * rows, cols),
        hidden.reshape(n * rows, cols),
        b_update.reshape(1, n),
        b_reset.reshape(1, n),
        b_cand.reshape(1, n),
        w_update,
        w_reset,
        w_cand,
    )
    return result.reshape(n, rows, cols)


def solution(mesh):
    in_specs = (
        P("chan", "rows", None),
        P("chan", "rows", None),
        P(None, None, "chan", None),
        P(None, None, "chan", None),
        P(None, None, "chan", None),
        P("chan"),
        P("chan"),
        P("chan"),
    )
    return jax.shard_map(
        functools.partial(per_device, mesh.shape["chan"], mesh.shape["rows"]),
        mesh=mesh,
        in_specs=in_specs,
        out_specs=P("chan", "rows", None),
        check_vma=False,
    )
```

```python
import functools

import jax
import jax.numpy as jnp
from jax import lax
from jax.experimental import pallas as pl
from jax.experimental.pallas import tpu as pltpu
from jax.sharding import PartitionSpec as P

MESH = pl.DeviceIdType.MESH
PAIR = 2
WIDE = 128
EDGE, INNER = 0, 1


def kernel(
    n_chan, n_rows, rows,
    features, hidden, b_update, b_reset, b_cand, w_update, w_reset, w_cand,
    out,
    raw, joined, rh, weights, acc, acc_cand, gate, bias,
    raw_sem, w_sem, send1, band1, rim1, send2, band2, rim2,
):
    cols = raw.shape[-1]
    channels = joined.shape[2]
    n = channels // n_chan
    lines = n_chan // PAIR
    me = lax.axis_index("chan")
    row = lax.axis_index("rows")
    line, pair = me // PAIR, me % PAIR
    has_up, has_down = line < lines - 1, line > 0
    has_above, has_below = row > 0, row < n_rows - 1
    eager = n % WIDE == 0
    f32 = jnp.float32

    raw_copies = [
        pltpu.make_async_copy(src, raw.at[i], raw_sem.at[i])
        for i, src in enumerate((features, hidden))
    ]
    w_copies = [
        pltpu.make_async_copy(src, weights.at[i], w_sem.at[i])
        for i, src in enumerate((w_reset, w_update, w_cand))
    ]
    for copy in raw_copies:
        copy.start()

    def ident(l, p):
        return l * PAIR + p

    up, down, partner = ident(line + 1, pair), ident(line - 1, pair), ident(line, 1 - pair)
    barrier = pltpu.get_barrier_semaphore()

    def greet(there, target):
        @pl.when(there)
        def _():
            pl.semaphore_signal(barrier, inc=1, device_id=target, device_id_type=MESH)

    pl.semaphore_signal(barrier, inc=1, device_id={"chan": partner}, device_id_type=MESH)
    greet(has_up, {"chan": up})
    greet(has_down, {"chan": down})
    greet(has_above, {"rows": row - 1})
    greet(has_below, {"rows": row + 1})

    def slot(r):
        if r == -1 or r == rows:
            return rows + (r == rows)
        return {0: 0, rows - 1: 1}.get(r, r + 1)

    def block(c):
        return pl.ds(pl.multiple_of(c * n, n), n)

    mine = block(me)

    def iota(shape, axis):
        return lax.broadcasted_iota(jnp.int32, shape, axis)

    to_planes = jnp.concatenate(
        [
            (iota((n, n * rows), 0) * rows + r == iota((n, n * rows), 1)).astype(f32)
            for r in range(rows)
        ],
        0,
    ).astype(raw.dtype)
    for copy in raw_copies:
        copy.wait()
    for copy in w_copies:
        copy.start()
    for i in range(2):
        planes = jnp.dot(to_planes, raw[i], preferred_element_type=f32).astype(raw.dtype)
        for r in range(rows):
            joined[i, slot(r), mine] = planes[r * n : (r + 1) * n]

    pl.semaphore_wait(
        barrier,
        1
        + has_up.astype(jnp.int32)
        + has_down.astype(jnp.int32)
        + has_above.astype(jnp.int32)
        + has_below.astype(jnp.int32),
    )

    class Mover:
        def __init__(self, buf, send, band_sem, rim_sem):
            self.buf, self.send, self.band_sem, self.rim_sem = buf, send, band_sem, rim_sem
            self.kinds = range(buf.shape[0])

        def band(self, way, c, part, h):
            slots = pl.ds(0, 2) if part == EDGE else pl.ds(2, rows - 2)
            ref = self.buf.at[h, slots, block(c)]
            return pltpu.make_async_remote_copy(
                src_ref=ref,
                dst_ref=ref,
                send_sem=self.send.at[way, c],
                recv_sem=self.band_sem.at[c, part, h],
                device_id={"chan": (up, down, partner)[way]},
                device_id_type=MESH,
            )

        def rim(self, side, c, h):
            return pltpu.make_async_remote_copy(
                src_ref=self.buf.at[h, side, block(c)],
                dst_ref=self.buf.at[h, rows + 1 - side, block(c)],
                send_sem=self.send.at[3 + side, c],
                recv_sem=self.rim_sem.at[side, c],
                device_id={"rows": row - 1 if side == 0 else row + 1},
                device_id_type=MESH,
            )

        def rims(self, c, h, act):
            @pl.when(has_above)
            def _():
                act(self.rim(0, c, h))

            @pl.when(has_below)
            def _():
                act(self.rim(1, c, h))

        def along(self, way, c, part, h, act):
            @pl.when((has_up, has_down)[way])
            def _():
                act(self.band(way, c, part, h))

        def begin(self, act, part):
            for h in self.kinds:
                self.along(0, me, part, h, act)
                self.along(1, me, part, h, act)
                act(self.band(2, me, part, h))
            if part == EDGE:
                for h in self.kinds:
                    self.rims(me, h, act)

        def pass_on(self, s, act, first):
            for part in (EDGE, INNER):
                for h in self.kinds:
                    for way, l in ((0, line - s), (1, line + s)):
                        @pl.when((l >= 0) & (l < lines))
                        def _():
                            c = ident(l, pair)
                            if first:
                                self.band(2, c, part, h).wait_recv()
                            self.along(way, c, part, h, act)
                            if part == EDGE or s > 1:
                                act(self.band(2, c, part, h))
                            if part == EDGE:
                                self.rims(c, h, act)

        def diagonal(self, act):
            for h in self.kinds:
                self.along(0, partner, INNER, h, act)
                self.along(1, partner, INNER, h, act)

        def across(self, s, act, first):
            for l in (line - s, line + s)[: 1 if s == 0 else 2]:
                @pl.when((l >= 0) & (l < lines))
                def _():
                    c = ident(l, 1 - pair)
                    for h in self.kinds:
                        if first:
                            self.band(2, c, EDGE, h).wait_recv()
                        self.rims(c, h, act)

        def all_of(self, sem, slots, c):
            ref = self.buf.at[:, slots, block(c)]
            return pltpu.make_async_copy(ref, ref, sem)

        def rims_in(self, c):
            for side, there in ((0, has_below), (1, has_above)):
                @pl.when(there)
                def _():
                    slots = pl.ds(rows + 1 - side, 1)
                    self.all_of(self.rim_sem.at[side, c], slots, c).wait()

        def inner_in(self, c):
            for h in self.kinds:
                self.band(2, c, INNER, h).wait_recv()

        def sent(self, way, slots, c):
            self.all_of(self.send.at[way, c], slots, c).wait()

        def finish(self):
            ways = ((has_up, 0), (has_down, 1))
            whole, edge, inner = pl.ds(0, rows), pl.ds(0, 2), pl.ds(2, rows - 2)
            for there, way in ways:
                @pl.when(there)
                def _():
                    self.sent(way, whole, me)
                    self.sent(way, inner, partner)
            self.sent(2, whole, me)
            for s in range(1, lines):
                for l, (there, way) in zip((line - s, line + s), ways):
                    c = ident(l, pair)

                    @pl.when((l >= 0) & (l < lines))
                    def _():
                        self.sent(2, edge if s == 1 else whole, c)

                    @pl.when((l >= 0) & (l < lines) & there)
                    def _():
                        self.sent(way, whole, c)

            @pl.loop(0, n_chan)
            def _(c):
                for there, side in ((has_above, 0), (has_below, 1)):
                    @pl.when(there)
                    def _():
                        self.sent(3 + side, pl.ds(side, 1), c)

    def start(copy):
        copy.start()

    def sides(s, body):
        @pl.loop(0, 2)
        def _(j):
            l = line + (2 * j - 1) * s

            @pl.when((l >= 0) & (l < lines))
            def _():
                body(l)

    first, second = Mover(joined, send1, band1, rim1), Mover(rh, send2, band2, rim2)
    for part in (EDGE, INNER):
        first.begin(start, part)

    for there, r in ((has_above, -1), (has_below, rows)):
        @pl.when(jnp.logical_not(there))
        def _():
            for buf in (joined, rh):
                for h in range(buf.shape[0]):
                    buf[h, slot(r)] = jnp.zeros((channels, cols), buf.dtype)

    diagonal = iota((n, n), 0) == iota((n, n), 1)
    for i, ref in enumerate((b_reset, b_update, b_cand)):
        column = jnp.sum(jnp.where(diagonal, ref[...], 0.0), axis=1, keepdims=True)
        bias[i] = jnp.broadcast_to(column, (n, cols))
    acc_cand[...] = jnp.zeros_like(acc_cand)
    if not eager:
        acc[...] = jnp.zeros_like(acc)

    def product(gates, count, sources, at, width):
        left, right = [], []
        for a in range(3):
            for offset, buf, h in sources:
                kw = pl.ds(pl.multiple_of(offset + at, WIDE), width)
                ks = pl.ds(pl.multiple_of(at, WIDE), width)
                left.append(
                    weights[pl.ds(gates, count), a, :, :, kw].reshape(count * 3 * n, width)
                )
                right.append(
                    jnp.concatenate([buf[h, slot(r + a - 1), ks] for r in range(rows)], 1)
                )
        return jnp.dot(
            jnp.concatenate(left, 1),
            jnp.concatenate(right, 0),
            preferred_element_type=f32,
        )

    both = ((0, joined, 0), (channels, joined, 1))
    size = 3 * n

    def gates_on(c):
        acc[...] += product(0, 2, both, c * n, n)

    def reset_on(c):
        acc[pl.ds(0, size)] += product(0, 1, both, c * n, n)

    def update_on(c):
        acc[pl.ds(size, size)] += product(1, 1, both, c * n, n)

    def old_on(at, width):
        acc_cand[...] += product(2, 1, ((0, joined, 0),), at, width)

    def new_on(at, width):
        acc_cand[...] += product(2, 1, ((channels, rh, 0),), at, width)

    last = sorted({1, lines - 1})

    def near(s):
        def body(l):
            c = ident(l, pair)
            first.rims_in(c)
            gates_on(c)

        sides(s, body)

    def far(s, compute):
        def body(l):
            c = ident(l, 1 - pair)
            first.inner_in(c)
            first.rims_in(c)
            compute(c)

        sides(s, body)

    for s in range(1, lines):
        first.pass_on(s, start, True)
        if s == max(1, lines - 2):
            if s == 1:
                first.inner_in(partner)
            first.diagonal(start)
        first.across(s - 1, start, True)
        if s == 1:
            if lines > 3:
                first.inner_in(partner)
            w_copies[0].wait()
            w_copies[1].wait()
            if eager:
                first.rims_in(me)
                acc[...] = product(0, 2, both, me * n, n)
                first.rims_in(partner)
                gates_on(partner)
        elif eager:
            near(s - 1)
            if s > 2:
                far(s - 1, gates_on)
    first.across(lines - 1, start, True)
    if eager:
        near(lines - 1)
        for s in last:
            far(s, reset_on)
    else:
        for s in range(1, lines):
            sides(s, lambda l: first.inner_in(ident(l, 1 - pair)))

        @pl.loop(0, n_chan)
        def _(c):
            first.rims_in(c)

        @pl.loop(0, channels // WIDE)
        def _(g):
            acc[...] += product(0, 2, both, g * WIDE, WIDE)

    lane = iota((n, cols), 1)

    def folded(ref, i, r):
        cells = pl.ds(r * cols, cols)
        low = pltpu.roll(ref[pl.ds(i * size, n), cells], 1, 1)
        mid = ref[pl.ds(i * size + n, n), cells]
        high = pltpu.roll(ref[pl.ds(i * size + 2 * n, n), cells], cols - 1, 1)
        return jnp.where(lane == 0, 0.0, low) + mid + jnp.where(lane == cols - 1, 0.0, high)

    def own_hidden(r):
        return joined[1, slot(r), mine].astype(f32)

    for part, inside in ((EDGE, (0, rows - 1)), (INNER, range(1, rows - 1))):
        for r in inside:
            reset = jax.nn.sigmoid(folded(acc, 0, r) + bias[0])
            rh[0, slot(r), mine] = (reset * own_hidden(r)).astype(rh.dtype)
        second.begin(start, part)

    if eager:
        for s in last:
            sides(s, lambda l: update_on(ident(l, 1 - pair)))
    w_copies[2].wait()

    def older():
        width = PAIR * n if eager else WIDE

        @pl.loop(0, channels // width)
        def _(g):
            old_on(g * width, width)

        for r in range(rows):
            gate[r] = jax.nn.sigmoid(folded(acc, 1, r) + bias[1])

    def both_on(l):
        for p in range(PAIR):
            second.rims_in(ident(l, p))
        new_on(l * PAIR * n, PAIR * n)

    def both_far(s):
        def body(l):
            second.inner_in(ident(l, 1 - pair))
            both_on(l)

        sides(s, body)

    for s in range(1, lines):
        second.pass_on(s, start, True)
        if s == max(1, lines - 2):
            if s == 1:
                second.inner_in(partner)
            second.diagonal(start)
        second.across(s - 1, start, True)
        if s == 1:
            if lines > 3:
                second.inner_in(partner)
            older()
            if eager:
                both_on(line)
        elif eager and s > 2:
            both_far(s - 1)
    second.across(lines - 1, start, True)
    if eager:
        for s in last:
            both_far(s)
    else:
        for s in range(1, lines):
            sides(s, lambda l: second.inner_in(ident(l, 1 - pair)))

        @pl.loop(0, n_chan)
        def _(c):
            second.rims_in(c)

        @pl.loop(0, channels // WIDE)
        def _(g):
            new_on(g * WIDE, WIDE)

    fresh = []
    for r in range(rows):
        candidate = jnp.tanh(folded(acc_cand, 0, r) + bias[2])
        update = gate[r]
        fresh.append(((1.0 - update) * own_hidden(r) + update * candidate).astype(out.dtype))
    from_planes = jnp.concatenate(
        [
            (iota((n * rows, n), 0) == iota((n * rows, n), 1) * rows + r).astype(f32)
            for r in range(rows)
        ],
        1,
    ).astype(out.dtype)
    out[...] = jnp.dot(
        from_planes, jnp.concatenate(fresh, 0), preferred_element_type=f32
    ).astype(out.dtype)
    first.finish()
    second.finish()


def per_device(n_chan, n_rows, features, hidden, w_update, w_reset, w_cand, b_update, b_reset, b_cand):
    n, rows, cols = features.shape
    band = rows * cols
    channels = n * n_chan
    bf16, f32 = jnp.bfloat16, jnp.float32
    vmem = pl.BlockSpec(memory_space=pltpu.VMEM)
    hbm = pl.BlockSpec(memory_space=pl.ANY)
    dma = pltpu.SemaphoreType.DMA
    result = pl.pallas_call(
        functools.partial(kernel, n_chan, n_rows, rows),
        out_shape=jax.ShapeDtypeStruct((n * rows, cols), bf16),
        in_specs=[hbm] * 2 + [vmem] * 3 + [hbm] * 3,
        out_specs=vmem,
        scratch_shapes=[
            pltpu.VMEM((2, n * rows, cols), bf16),
            pltpu.VMEM((2, rows + 2, channels, cols), bf16),
            pltpu.VMEM((1, rows + 2, channels, cols), bf16),
            pltpu.VMEM((3,) + w_update.shape, bf16),
            pltpu.VMEM((6 * n, band), f32),
            pltpu.VMEM((3 * n, band), f32),
            pltpu.VMEM((rows, n, cols), f32),
            pltpu.VMEM((3, n, cols), f32),
            dma((2,)),
            dma((3,)),
            dma((5, n_chan)),
            dma((n_chan, 2, 2)),
            dma((2, n_chan)),
            dma((5, n_chan)),
            dma((n_chan, 2, 1)),
            dma((2, n_chan)),
        ],
        compiler_params=pltpu.CompilerParams(
            collective_id=0, has_side_effects=True, vmem_limit_bytes=60 * 1024 * 1024
        ),
    )(
        features.reshape(n * rows, cols),
        hidden.reshape(n * rows, cols),
        b_update.reshape(1, n),
        b_reset.reshape(1, n),
        b_cand.reshape(1, n),
        w_update,
        w_reset,
        w_cand,
    )
    return result.reshape(n, rows, cols)


def solution(mesh):
    in_specs = (
        P("chan", "rows", None),
        P("chan", "rows", None),
        P(None, None, "chan", None),
        P(None, None, "chan", None),
        P(None, None, "chan", None),
        P("chan"),
        P("chan"),
        P("chan"),
    )
    return jax.shard_map(
        functools.partial(per_device, mesh.shape["chan"], mesh.shape["rows"]),
        mesh=mesh,
        in_specs=in_specs,
        out_specs=P("chan", "rows", None),
        check_vma=False,
    )
```

```python
import functools

import jax
import jax.numpy as jnp
from jax import lax
from jax.experimental import pallas as pl
from jax.experimental.pallas import tpu as pltpu
from jax.sharding import PartitionSpec as P

MESH = pl.DeviceIdType.MESH
PAIR = 2
WIDE = 128
EDGE, INNER = 0, 1


def kernel(
    n_chan, n_rows, rows,
    features, hidden, b_update, b_reset, b_cand, w_update, w_reset, w_cand,
    out,
    raw, joined, rh, weights, acc, acc_cand, gate, bias,
    raw_sem, w_sem, send1, band1, rim1, send2, band2, rim2,
):
    cols = raw.shape[-1]
    channels = joined.shape[2]
    n = channels // n_chan
    lines = n_chan // PAIR
    me = lax.axis_index("chan")
    row = lax.axis_index("rows")
    line, pair = me // PAIR, me % PAIR
    has_up, has_down = line < lines - 1, line > 0
    at_end = (line == 0) | (line == lines - 1)
    has_above, has_below = row > 0, row < n_rows - 1
    eager = n % WIDE == 0
    f32 = jnp.float32

    raw_copies = [
        pltpu.make_async_copy(src, raw.at[i], raw_sem.at[i])
        for i, src in enumerate((features, hidden))
    ]
    w_copies = [
        pltpu.make_async_copy(src, weights.at[i], w_sem.at[i])
        for i, src in enumerate((w_reset, w_update, w_cand))
    ]
    for copy in raw_copies:
        copy.start()

    def ident(l, p):
        return l * PAIR + p

    up, down, partner = ident(line + 1, pair), ident(line - 1, pair), ident(line, 1 - pair)
    far_end = ident(lines - 1 - line, pair)
    to_far = at_end if lines > 2 else line < 0
    barrier = pltpu.get_barrier_semaphore()

    def greet(there, target):
        @pl.when(there)
        def _():
            pl.semaphore_signal(barrier, inc=1, device_id=target, device_id_type=MESH)

    pl.semaphore_signal(barrier, inc=1, device_id={"chan": partner}, device_id_type=MESH)
    greet(has_up, {"chan": up})
    greet(has_down, {"chan": down})
    greet(to_far, {"chan": far_end})
    greet(has_above, {"rows": row - 1})
    greet(has_below, {"rows": row + 1})

    def slot(r):
        if r == -1 or r == rows:
            return rows + (r == rows)
        return {0: 0, rows - 1: 1}.get(r, r + 1)

    def block(c):
        return pl.ds(pl.multiple_of(c * n, n), n)

    mine = block(me)

    def iota(shape, axis):
        return lax.broadcasted_iota(jnp.int32, shape, axis)

    to_planes = jnp.concatenate(
        [
            (iota((n, n * rows), 0) * rows + r == iota((n, n * rows), 1)).astype(f32)
            for r in range(rows)
        ],
        0,
    ).astype(raw.dtype)
    for copy in raw_copies:
        copy.wait()
    for copy in w_copies:
        copy.start()
    for i in range(2):
        planes = jnp.dot(to_planes, raw[i], preferred_element_type=f32).astype(raw.dtype)
        for r in range(rows):
            joined[i, slot(r), mine] = planes[r * n : (r + 1) * n]

    pl.semaphore_wait(
        barrier,
        1
        + has_up.astype(jnp.int32)
        + has_down.astype(jnp.int32)
        + to_far.astype(jnp.int32)
        + has_above.astype(jnp.int32)
        + has_below.astype(jnp.int32),
    )

    class Mover:
        def __init__(self, buf, send, band_sem, rim_sem):
            self.buf, self.send, self.band_sem, self.rim_sem = buf, send, band_sem, rim_sem
            self.kinds = range(2)

        def half(self, slots, c, h):
            if self.buf.shape[0] == 2:
                return self.buf.at[h, slots, block(c)]
            few = n // 2
            return self.buf.at[0, slots, pl.ds(pl.multiple_of(c * n + h * few, few), few)]

        def band(self, way, c, part, h, target=None):
            slots = pl.ds(0, 2) if part == EDGE else pl.ds(2, rows - 2)
            ref = self.half(slots, c, h)
            return pltpu.make_async_remote_copy(
                src_ref=ref,
                dst_ref=ref,
                send_sem=self.send.at[way, c],
                recv_sem=self.band_sem.at[c, part, h],
                device_id={"chan": (up, down, partner)[way] if target is None else target},
                device_id_type=MESH,
            )

        def rim(self, side, c, h):
            return pltpu.make_async_remote_copy(
                src_ref=self.half(pl.ds(side, 1), c, h),
                dst_ref=self.half(pl.ds(rows + 1 - side, 1), c, h),
                send_sem=self.send.at[3 + side, c],
                recv_sem=self.rim_sem.at[side, c],
                device_id={"rows": row - 1 if side == 0 else row + 1},
                device_id_type=MESH,
            )

        def rims(self, c, h, act):
            @pl.when(has_above)
            def _():
                act(self.rim(0, c, h))

            @pl.when(has_below)
            def _():
                act(self.rim(1, c, h))

        def along(self, way, c, part, h, act):
            @pl.when((has_up, has_down)[way])
            def _():
                act(self.band(way, c, part, h))

        def begin(self, act, part):
            for h in self.kinds:
                self.along(0, me, part, h, act)
                self.along(1, me, part, h, act)
                act(self.band(2, me, part, h))
            if part == EDGE:
                for h in self.kinds:
                    self.rims(me, h, act)

        def pass_on(self, s, part, act):
            for h in self.kinds:
                for way, l, end in ((0, line - s, 0), (1, line + s, lines - 1)):
                    c = ident(l, pair)
                    there = (l >= 0) & (l < lines)

                    @pl.when(there)
                    def _():
                        self.band(2, c, part, h).wait_recv()
                        self.along(way, c, part, h, act)
                        if part == INNER or s not in (1, lines - 1):
                            act(self.band(2, c, part, h))

                    if part == EDGE and s == 1 and lines > 2:
                        @pl.when(there & (l != end))
                        def _():
                            act(self.band(2, c, part, h))

                    if part == EDGE:
                        @pl.when(there)
                        def _():
                            self.rims(c, h, act)

        def diagonal(self, act):
            for h in self.kinds:
                for way, end in ((0, 0), (1, lines - 1)):
                    @pl.when(line == end)
                    def _():
                        act(self.band(way, partner, EDGE, h))
                        if lines > 2:
                            act(self.band(1 - way, partner, EDGE, h, far_end))

        def across(self, s, act):
            for l in (line - s, line + s)[: 1 if s == 0 else 2]:
                @pl.when((l >= 0) & (l < lines))
                def _():
                    c = ident(l, 1 - pair)
                    for h in self.kinds:
                        self.band(2, c, EDGE, h).wait_recv()
                        self.rims(c, h, act)

        def all_of(self, sem, slots, c):
            ref = self.buf.at[:, slots, block(c)]
            return pltpu.make_async_copy(ref, ref, sem)

        def rims_in(self, c):
            for side, there in ((0, has_below), (1, has_above)):
                @pl.when(there)
                def _():
                    slots = pl.ds(rows + 1 - side, 1)
                    self.all_of(self.rim_sem.at[side, c], slots, c).wait()

        def inner_in(self, c):
            for h in self.kinds:
                self.band(2, c, INNER, h).wait_recv()

        def sent(self, way, slots, c):
            self.all_of(self.send.at[way, c], slots, c).wait()

        def finish(self):
            ways = ((has_up, 0), (has_down, 1))
            whole, edge, inner = pl.ds(0, rows), pl.ds(0, 2), pl.ds(2, rows - 2)
            for there, way in ways:
                @pl.when(there)
                def _():
                    self.sent(way, whole, me)

                @pl.when(at_end if lines > 2 else at_end & there)
                def _():
                    self.sent(way, edge, partner)
            self.sent(2, whole, me)
            for s in range(1, lines):
                for l, end, (there, way) in zip((line - s, line + s), (0, lines - 1), ways):
                    c = ident(l, pair)
                    short = l == end if s in (1, lines - 1) else l < 0

                    @pl.when((l >= 0) & (l < lines) & short)
                    def _():
                        self.sent(2, inner, c)

                    @pl.when((l >= 0) & (l < lines) & jnp.logical_not(short))
                    def _():
                        self.sent(2, whole, c)

                    @pl.when((l >= 0) & (l < lines) & there)
                    def _():
                        self.sent(way, whole, c)

            @pl.loop(0, n_chan)
            def _(c):
                for there, side in ((has_above, 0), (has_below, 1)):
                    @pl.when(there)
                    def _():
                        self.sent(3 + side, pl.ds(side, 1), c)

    def start(copy):
        copy.start()

    def sides(s, body):
        @pl.loop(0, 2)
        def _(j):
            l = line + (2 * j - 1) * s

            @pl.when((l >= 0) & (l < lines))
            def _():
                body(l)

    first, second = Mover(joined, send1, band1, rim1), Mover(rh, send2, band2, rim2)
    for part in (EDGE, INNER):
        first.begin(start, part)

    for there, r in ((has_above, -1), (has_below, rows)):
        @pl.when(jnp.logical_not(there))
        def _():
            for buf in (joined, rh):
                for h in range(buf.shape[0]):
                    buf[h, slot(r)] = jnp.zeros((channels, cols), buf.dtype)

    diagonal = iota((n, n), 0) == iota((n, n), 1)
    for i, ref in enumerate((b_reset, b_update, b_cand)):
        column = jnp.sum(jnp.where(diagonal, ref[...], 0.0), axis=1, keepdims=True)
        bias[i] = jnp.broadcast_to(column, (n, cols))
    acc_cand[...] = jnp.zeros_like(acc_cand)
    if not eager:
        acc[...] = jnp.zeros_like(acc)

    def product(gates, count, sources, at, width):
        left, right = [], []
        for a in range(3):
            for offset, buf, h in sources:
                kw = pl.ds(pl.multiple_of(offset + at, WIDE), width)
                ks = pl.ds(pl.multiple_of(at, WIDE), width)
                left.append(
                    weights[pl.ds(gates, count), a, :, :, kw].reshape(count * 3 * n, width)
                )
                right.append(
                    jnp.concatenate([buf[h, slot(r + a - 1), ks] for r in range(rows)], 1)
                )
        return jnp.dot(
            jnp.concatenate(left, 1),
            jnp.concatenate(right, 0),
            preferred_element_type=f32,
        )

    both = ((0, joined, 0), (channels, joined, 1))
    size = 3 * n

    def gates_on(c):
        acc[...] += product(0, 2, both, c * n, n)

    def reset_on(c):
        acc[pl.ds(0, size)] += product(0, 1, both, c * n, n)

    def update_on(c):
        acc[pl.ds(size, size)] += product(1, 1, both, c * n, n)

    def old_on(at, width):
        acc_cand[...] += product(2, 1, ((0, joined, 0),), at, width)

    def new_on(at, width):
        acc_cand[...] += product(2, 1, ((channels, rh, 0),), at, width)

    def near(s, compute):
        def body(l):
            c = ident(l, pair)
            first.rims_in(c)
            compute(c)

        sides(s, body)

    def far(s, compute):
        def body(l):
            c = ident(l, 1 - pair)
            first.inner_in(c)
            first.rims_in(c)
            compute(c)

        sides(s, body)

    for s in range(1, lines):
        first.pass_on(s, EDGE, start)
        first.across(s - 1, start)
        if s == 1:
            first.diagonal(start)
        if s == lines - 1:
            first.across(s, start)
        first.pass_on(s, INNER, start)
        if s == 1:
            first.inner_in(partner)
            w_copies[0].wait()
            w_copies[1].wait()
            if eager:
                first.rims_in(me)
                acc[...] = product(0, 2, both, me * n, n)
                first.rims_in(partner)
                gates_on(partner)
        elif eager:
            near(s - 1, gates_on)
            far(s - 1, gates_on)
    if eager:
        near(lines - 1, reset_on)
        far(lines - 1, reset_on)
    else:
        for s in range(1, lines):
            sides(s, lambda l: first.inner_in(ident(l, 1 - pair)))

        @pl.loop(0, n_chan)
        def _(c):
            first.rims_in(c)

        @pl.loop(0, channels // WIDE)
        def _(g):
            acc[...] += product(0, 2, both, g * WIDE, WIDE)

    lane = iota((n, cols), 1)

    def folded(ref, i, r):
        cells = pl.ds(r * cols, cols)
        low = pltpu.roll(ref[pl.ds(i * size, n), cells], 1, 1)
        mid = ref[pl.ds(i * size + n, n), cells]
        high = pltpu.roll(ref[pl.ds(i * size + 2 * n, n), cells], cols - 1, 1)
        return jnp.where(lane == 0, 0.0, low) + mid + jnp.where(lane == cols - 1, 0.0, high)

    def own_hidden(r):
        return joined[1, slot(r), mine].astype(f32)

    for part, inside in ((EDGE, (0, rows - 1)), (INNER, range(1, rows - 1))):
        for r in inside:
            reset = jax.nn.sigmoid(folded(acc, 0, r) + bias[0])
            rh[0, slot(r), mine] = (reset * own_hidden(r)).astype(rh.dtype)
        second.begin(start, part)

    if eager:
        @pl.loop(0, PAIR)
        def _(p):
            sides(lines - 1, lambda l: update_on(ident(l, p)))
    w_copies[2].wait()
    width = PAIR * n if eager else WIDE

    @pl.loop(0, channels // width)
    def _(g):
        old_on(g * width, width)

    for r in range(rows):
        gate[r] = jax.nn.sigmoid(folded(acc, 1, r) + bias[1])

    def both_on(l):
        for p in range(PAIR):
            second.rims_in(ident(l, p))
        new_on(l * PAIR * n, PAIR * n)

    def both_far(s):
        def body(l):
            second.inner_in(ident(l, 1 - pair))
            both_on(l)

        sides(s, body)

    for s in range(1, lines):
        second.pass_on(s, EDGE, start)
        second.across(s - 1, start)
        if s == 1:
            second.diagonal(start)
        if s == lines - 1:
            second.across(s, start)
        second.pass_on(s, INNER, start)
        if s == 1:
            second.inner_in(partner)
        if not eager:
            continue
        if s == 1:
            both_on(line)
        else:
            both_far(s - 1)
    if eager:
        both_far(lines - 1)
    else:
        for s in range(1, lines):
            sides(s, lambda l: second.inner_in(ident(l, 1 - pair)))

        @pl.loop(0, n_chan)
        def _(c):
            second.rims_in(c)

        @pl.loop(0, channels // WIDE)
        def _(g):
            new_on(g * WIDE, WIDE)

    fresh = []
    for r in range(rows):
        candidate = jnp.tanh(folded(acc_cand, 0, r) + bias[2])
        update = gate[r]
        fresh.append(((1.0 - update) * own_hidden(r) + update * candidate).astype(out.dtype))
    from_planes = jnp.concatenate(
        [
            (iota((n * rows, n), 0) == iota((n * rows, n), 1) * rows + r).astype(f32)
            for r in range(rows)
        ],
        1,
    ).astype(out.dtype)
    out[...] = jnp.dot(
        from_planes, jnp.concatenate(fresh, 0), preferred_element_type=f32
    ).astype(out.dtype)
    first.finish()
    second.finish()


def per_device(n_chan, n_rows, features, hidden, w_update, w_reset, w_cand, b_update, b_reset, b_cand):
    n, rows, cols = features.shape
    band = rows * cols
    channels = n * n_chan
    bf16, f32 = jnp.bfloat16, jnp.float32
    vmem = pl.BlockSpec(memory_space=pltpu.VMEM)
    hbm = pl.BlockSpec(memory_space=pl.ANY)
    dma = pltpu.SemaphoreType.DMA
    result = pl.pallas_call(
        functools.partial(kernel, n_chan, n_rows, rows),
        out_shape=jax.ShapeDtypeStruct((n * rows, cols), bf16),
        in_specs=[hbm] * 2 + [vmem] * 3 + [hbm] * 3,
        out_specs=vmem,
        scratch_shapes=[
            pltpu.VMEM((2, n * rows, cols), bf16),
            pltpu.VMEM((2, rows + 2, channels, cols), bf16),
            pltpu.VMEM((1, rows + 2, channels, cols), bf16),
            pltpu.VMEM((3,) + w_update.shape, bf16),
            pltpu.VMEM((6 * n, band), f32),
            pltpu.VMEM((3 * n, band), f32),
            pltpu.VMEM((rows, n, cols), f32),
            pltpu.VMEM((3, n, cols), f32),
            dma((2,)),
            dma((3,)),
            dma((5, n_chan)),
            dma((n_chan, 2, 2)),
            dma((2, n_chan)),
            dma((5, n_chan)),
            dma((n_chan, 2, 2)),
            dma((2, n_chan)),
        ],
        compiler_params=pltpu.CompilerParams(
            collective_id=0, has_side_effects=True, vmem_limit_bytes=60 * 1024 * 1024
        ),
    )(
        features.reshape(n * rows, cols),
        hidden.reshape(n * rows, cols),
        b_update.reshape(1, n),
        b_reset.reshape(1, n),
        b_cand.reshape(1, n),
        w_update,
        w_reset,
        w_cand,
    )
    return result.reshape(n, rows, cols)


def solution(mesh):
    in_specs = (
        P("chan", "rows", None),
        P("chan", "rows", None),
        P(None, None, "chan", None),
        P(None, None, "chan", None),
        P(None, None, "chan", None),
        P("chan"),
        P("chan"),
        P("chan"),
    )
    return jax.shard_map(
        functools.partial(per_device, mesh.shape["chan"], mesh.shape["rows"]),
        mesh=mesh,
        in_specs=in_specs,
        out_specs=P("chan", "rows", None),
        check_vma=False,
    )
```
